32 devices in a mesh: sample: 2 (over y), harm: 16 (over z, x, core).
Axes of the slice: x: 2, y: 2, z: 4, core: 2. Of those that a mesh axis runs over, the one named last changes fastest.
Arguments:
- inputs: bfloat16 [128, 64, 512], P('sample', 'harm'), parts along dimension 0, may hold values from -6 to 6
- col_list: int32 [128], P('sample'), parts along dimension 0, may hold values from 0 to 63, each once
- row_list: int32 [128], P('sample'), parts along dimension 0, may hold values from 0 to 63, each once
- gain_attn: float32 [512], replicated, may hold values from 0.25 to 1.75
- w_qkv: bfloat16 [512, 1536], replicated
- w_out: bfloat16 [512, 512], replicated, may hold values from -0.25 to 0.25
- gain_ffn: float32 [512], replicated, may hold values from 0.25 to 1.75
- w_gate: bfloat16 [512, 1024], P('harm'), may hold values from -0.25 to 0.25
- w_up: bfloat16 [512, 1024], P('harm'), may hold values from -0.25 to 0.25
- w_down: bfloat16 [1024, 512], P('harm'), may hold values from -0.1875 to 0.1875
Outputs:
- result: bfloat16 [64, 128, 512], P('harm', 'sample'), parts along dimension 1
The draws below stay inside these ranges and needn't reach their ends.
There are 2 independent parts, one for each index of `sample`. The reference program is written for one: setup_inputs(seed, part) draws one part's arguments, and reference() takes and returns one part's arrays. A program takes and returns all parts, laid end to end along the dimension named above; an argument that names none is the same for every part. Nothing has to cross between parts.
Inputs may be any that keep to these rules, and one draw needn't show every extreme that they name: col_list names every order m of 0 to 63 exactly once. row_list names every degree ell of 0 to 63 exactly once.
All inputs are finite; a program needn't handle non-finite values.
Results may differ from the reference program's by a relative error of at most 0.0073.
Values may be sent and summed in bfloat16 or wider, within the bound.
A program may use at most 64 MiB of HBM per device.

```python
import jax
import jax.numpy as jnp
from jax import lax

D = 512
HEADS = 8
FF = 1024
WIN = 256
LMAX = 64


def draw_w_qkv(key, part):
    first = jax.random.fold_in(key, 0)
    base = jax.random.normal(first, (D, 3 * D), jnp.float32) * (2.0 / D) ** 0.5
    return base.astype(jnp.bfloat16)


def shard_levels(rng, extent, shards, least, high):
    def one(position, shards_of):
        draws = jax.random.uniform(jax.random.fold_in(jax.random.fold_in(rng, 6), position), (shards_of,), jnp.float32, least / len(shards), high / len(shards))
        return jnp.repeat(jnp.exp(draws), extent[position] // shards_of).reshape((-1,) + (1,) * (len(extent) - position - 1))

    factor_of = one(*shards[0])
    for cut in shards[1:]:
        factor_of = factor_of * one(*cut)
    return factor_of


def centred(key, shape, width, most, pieces=(), kind=jnp.bfloat16):
    values = jax.random.normal(key, shape, jnp.float32) * width
    if len(pieces) > 0:
        values = shard_levels(key, shape, pieces, -0.22, 0.18) * values
    return jnp.clip(values, min=-most, max=most).astype(kind)


def setup_inputs(seed: int = 0, part: int = 0) -> dict:
    streams_of = jax.random.split(jax.random.key(seed), 11)
    part_keys = jax.random.split(jax.random.fold_in(streams_of[10], part), 11)
    inputs = centred(part_keys[0], (LMAX, LMAX, D), 1.0, 6.0, ((1, 16),))
    col_list = jax.random.permutation(part_keys[1], LMAX).astype(jnp.int32)
    row_list = jax.random.permutation(part_keys[2], LMAX).astype(jnp.int32)
    gain_attn = jnp.clip(1.0 + 0.15 * jax.random.normal(streams_of[3], (D,), jnp.float32), 0.25, 1.75)
    w_qkv = draw_w_qkv(jax.random.fold_in(streams_of[10], 71), part)
    w_out = centred(streams_of[5], (D, D), D ** -0.5, 0.25)
    gain_ffn = jnp.clip(1.0 + 0.15 * jax.random.normal(streams_of[6], (D,), jnp.float32), 0.25, 1.75)
    w_gate = centred(streams_of[7], (D, FF), D ** -0.5, 0.25, ((0, 16),))
    w_up = centred(streams_of[8], (D, FF), D ** -0.5, 0.25, ((0, 16),))
    w_down = centred(streams_of[9], (FF, D), FF ** -0.5, 0.1875, ((0, 16),))
    return {"inputs": inputs, "col_list": col_list, "row_list": row_list, "gain_attn": gain_attn, "w_qkv": w_qkv, "w_out": w_out, "gain_ffn": gain_ffn, "w_gate": w_gate, "w_up": w_up, "w_down": w_down}


eps = 1e-06
masked = -1e+30
exact = lax.Precision.HIGHEST

def rms_scale(values, gain):
    values = values.astype(jnp.float32)
    mean_sq = lax.optimization_barrier(jnp.mean(values * values, axis=-1, keepdims=True))
    return values * lax.rsqrt(mean_sq + eps) * gain.astype(jnp.float32)

def attend(query, keys, values, allowed, scale):
    scores = jnp.einsum('lhd,khd->hlk', query.astype(jnp.float32), keys.astype(jnp.float32), precision=exact) * scale
    scores = jnp.where(allowed[None], scores, masked)
    top = lax.optimization_barrier(jnp.max(scores, axis=-1, keepdims=True))
    weights = jnp.exp(scores - top)
    probs = (weights / lax.optimization_barrier(jnp.sum(weights, axis=-1, keepdims=True))).astype(jnp.bfloat16)
    mixed = jnp.einsum('hlk,khd->lhd', probs.astype(jnp.float32), values.astype(jnp.float32), precision=exact)
    return mixed.astype(jnp.bfloat16)

def reference(inputs, col_list, row_list, gain_attn, w_qkv, w_out, gain_ffn, w_gate, w_up, w_down):
    head_dim = D // HEADS
    half = HEADS // 2
    split = half * head_dim
    scale = head_dim ** (-0.5)
    normed = rms_scale(inputs, gain_attn).astype(jnp.bfloat16)
    qkv = jnp.dot(normed.reshape(LMAX * LMAX, D), w_qkv, preferred_element_type=jnp.float32)
    qkv = qkv.astype(jnp.bfloat16).reshape(LMAX, LMAX, 3 * D)

    def heads_of(start):
        return qkv[:, :, start:start + split].reshape(LMAX, LMAX, half, head_dim)
    q_ell, k_ell, v_ell = (heads_of(0), heads_of(D), heads_of(2 * D))
    q_m, k_m, v_m = (heads_of(split), heads_of(D + split), heads_of(2 * D + split))
    here = jnp.arange(LMAX, dtype=jnp.int32)
    offset = here[None, :] - here[:, None]
    band = (offset >= -(WIN // 2)) & (offset < WIN // 2)

    def column(args):
        query, keys, values, start = args
        allowed = band & (here[None, :] >= start)
        return attend(query, keys, values, allowed, scale)
    a_ell = lax.map(column, (jnp.swapaxes(q_ell, 0, 1), jnp.swapaxes(k_ell, 0, 1), jnp.swapaxes(v_ell, 0, 1), col_list.astype(jnp.int32)))
    a_ell = jnp.swapaxes(a_ell, 0, 1)
    diff = col_list[None, :] - col_list[:, None]
    mband = (diff >= -(WIN // 2)) & (diff < WIN // 2)

    def row(args):
        query, keys, values, level = args
        allowed = mband & (col_list[None, :] <= level)
        return attend(query, keys, values, allowed, scale)
    a_m = lax.map(row, (q_m, k_m, v_m, here))
    attn = jnp.concatenate([a_ell.reshape(LMAX, LMAX, split), a_m.reshape(LMAX, LMAX, split)], axis=-1)
    resid = inputs.astype(jnp.float32) + jnp.dot(attn.reshape(LMAX * LMAX, D), w_out, preferred_element_type=jnp.float32).reshape(LMAX, LMAX, D)
    normed_ffn = rms_scale(resid, gain_ffn).astype(jnp.bfloat16).reshape(LMAX * LMAX, D)
    gate = jnp.dot(normed_ffn, w_gate, preferred_element_type=jnp.float32)
    up = jnp.dot(normed_ffn, w_up, preferred_element_type=jnp.float32)
    hidden = (jax.nn.silu(gate) * up).astype(jnp.bfloat16)
    final = resid + jnp.dot(hidden, w_down, preferred_element_type=jnp.float32).reshape(LMAX, LMAX, D)
    final = jnp.take(final, row_list.astype(jnp.int32), axis=0)
    valid = col_list[None, :] <= row_list[:, None]
    return jnp.where(valid[:, :, None], final, 0.0).astype(jnp.bfloat16)
```

```python
import functools

import jax
import jax.numpy as jnp
from jax import lax
from jax.experimental import pallas as pl
from jax.experimental.pallas import tpu as pltpu
from jax.sharding import PartitionSpec as P

HEADS = 8
WIN = 256
VMEM_MIB = 40
MESH = pl.DeviceIdType.MESH

eps = 1e-06
masked = -1e30


def rms_scale(values, gain):
    values = values.astype(jnp.float32)
    mean_sq = jnp.mean(values * values, axis=-1, keepdims=True)
    return values * lax.rsqrt(mean_sq + eps) * gain


def dot(a, b):
    return jnp.dot(a, b, preferred_element_type=jnp.float32)


def attention(query, keys, values, allowed, pair):
    low = lax.broadcasted_iota(jnp.int32, query.shape, 1) < pair // 2
    zero = jnp.zeros_like(query)
    mixed = []
    for part in (jnp.where(low, query, zero), jnp.where(low, zero, query)):
        scores = lax.dot_general(part, keys, (((1,), (1,)), ((), ())), preferred_element_type=jnp.float32)
        scores = jnp.where(allowed, scores, masked)
        top = jnp.max(scores, axis=-1, keepdims=True)
        weights = jnp.exp(scores - top)
        total = jnp.sum(weights, axis=-1, keepdims=True)
        mixed.append(dot(weights.astype(jnp.bfloat16), values) * (1.0 / total))
    return jnp.where(low, mixed[0], mixed[1])


def low_bit(d):
    return d & -d


def kernel(
    n, x_hbm, rows_smem, col_ref, row_ref, gain_a_ref, w_qkv_hbm, w_out_hbm, gain_f_ref, gate_hbm, up_hbm, down_hbm,
    out_ref, w_qkv_ref, w_out_ref, l_sem, mc_ref, mr_ref, x_ref, sent, ell_out, q_buf, k_buf, v_buf, got, got_ell, attn_m, gu, dn,
    sx_send, sx_recv, sa_send, sa_recv, z_send, z_recv, x_send, x_recv, y_send, y_recv, c_send, c_recv,
):
    me = lax.axis_index("harm")
    sample = lax.axis_index("sample")
    part = sample % 2
    other_plane = {"sample": sample + 1 - 2 * part, "harm": me}
    outer = n // 4
    zc, inner = me // 4, me % 4
    side, core = inner // 2, inner % 2
    other_side = {"harm": zc * 4 + (1 - side) * 2 + core}
    other_core = {"harm": zc * 4 + side * 2 + (1 - core)}
    depth = gate_hbm.shape[0]
    deep = down_hbm.shape[0]
    length, cols, width = x_ref.shape
    rows_here = length // n
    tokens = length * cols
    split = width // 2
    head_dim = width // HEADS
    pair = 2 * head_dim
    scale = head_dim ** (-0.5)
    step = min(tokens, 256)

    own_gu = pl.ds(pl.multiple_of(me * depth, depth), depth)
    own_dn = pl.ds(pl.multiple_of(me * deep, deep), deep)
    fetches = [
        pltpu.make_async_copy(a, b, l_sem.at[k])
        for k, (a, b) in enumerate((
            (x_hbm, x_ref), (gate_hbm, gu.at[0, own_gu, :]), (up_hbm, gu.at[1, own_gu, :]), (down_hbm, dn.at[own_dn, :]),
            (w_qkv_hbm, w_qkv_ref), (w_out_hbm, w_out_ref),
        ))
    ]
    for fetch in fetches:
        fetch.start()
    barrier = pltpu.get_barrier_semaphore()
    for d in range(1, n):
        pl.semaphore_signal(barrier, inc=1, device_id={"harm": (me + d) % n}, device_id_type=MESH)
    pl.semaphore_signal(barrier, inc=1, device_id=other_plane, device_id_type=MESH)

    def across(z, d):
        for b in [1 << i for i in range(outer.bit_length())]:
            if d & b:
                z = z + b * (1 - 2 * ((z // b) % 2))
        return z

    def place(z, s, c):
        return z * 4 + s * 2 + c

    def piece(k, i, half):
        size = (depth, deep)[k]
        first, rows = i * size, size
        if half is not None:
            rows = size // 2
            first = first + half * rows
        where = pl.ds(pl.multiple_of(first, rows), rows)
        return gu.at[:, where, :] if k == 0 else dn.at[where, :]

    pending = []

    def copy_of(k, i, half, send, recv, slot, device):
        view = piece(k, i, half)
        return pltpu.make_async_remote_copy(
            src_ref=view, dst_ref=view, send_sem=send.at[slot, k], recv_sem=recv.at[slot, k],
            device_id=device, device_id_type=MESH,
        )

    def push(*args):
        copy_of(*args).start()
        pending.append(lambda: copy_of(*args))

    def z_half(d):
        return None if d <= 1 else part

    def x_half(d):
        return None if d == 1 else part

    def z_push(d, b, k):
        device = {"harm": across(zc, b) * 4 + inner}
        push(k, place(across(zc, d), side, core), z_half(d | b), z_send, z_recv, d | b, device)

    def x_push(d, k):
        push(k, place(across(zc, d), side, core), x_half(d), x_send, x_recv, d, other_side)

    def y_push(other, d, k):
        s = 1 - side if other else side
        push(k, place(across(zc, d), s, core), part, y_send, y_recv, other * outer + d, other_plane)

    def c_args(kind, d, k, c):
        s = 1 - side if kind % 2 else side
        half = (z_half(d), x_half(d))[kind] if kind < 2 else 1 - part
        return k, place(across(zc, d), s, c), half, c_send, c_recv, kind * outer + d, other_core

    def c_push(kind, d, k):
        push(*c_args(kind, d, k, core))

    def halvings(d):
        top = outer if d == 0 else low_bit(d)
        return [b for b in reversed([1 << i for i in range(outer.bit_length())]) if b < top]

    def on_z(d, k):
        copy_of(k, place(across(zc, d), side, core), z_half(d), z_send, z_recv, d, other_core).wait_recv()
        for b in halvings(d):
            z_push(d, b, k)
        x_push(d, k)
        if d >= 2:
            y_push(0, d, k)
        c_push(0, d, k)

    def on_x(d, k):
        half = x_half(d)
        copy_of(k, place(across(zc, d), 1 - side, core), half, x_send, x_recv, d, other_side).wait_recv()
        if half is not None:
            y_push(1, d, k)
        c_push(1, d, k)

    def on_y(other, d, k):
        s = 1 - side if other else side
        slot = other * outer + d
        copy_of(k, place(across(zc, d), s, core), 1 - part, y_send, y_recv, slot, other_plane).wait_recv()
        c_push(2 + other, d, k)

    def on_core(k):
        for d in range(outer):
            for kind in range(4):
                if kind == 2 and d < 2 or kind == 3 and x_half(d) is None:
                    continue
                copy_of(*c_args(kind, d, k, 1 - core)).wait_recv()

    def to_row(src, dst, send, recv, d):
        peer = (me + d) % n
        return pltpu.make_async_remote_copy(
            src_ref=src.at[pl.ds(peer * rows_here, rows_here)], dst_ref=dst.at[:, me],
            send_sem=send.at[d], recv_sem=recv.at[d], device_id={"harm": peer}, device_id_type=MESH,
        )

    def tokens_out(src, dst, send, recv):
        for d in range(1, n):
            to_row(src, dst, send, recv, d).start()
            pending.append(lambda d=d: to_row(src, dst, send, recv, d))
        dst[:, me] = src[pl.ds(me * rows_here, rows_here)]

    def tokens_in(src, dst, send, recv):
        for d in range(1, n):
            to_row(src, dst, send, recv, d).wait_recv()

    fetches[0].wait()

    def order(slot, carry):
        sent[slot] = x_ref[rows_smem[slot]]
        return carry

    lax.fori_loop(0, length, order, 0, unroll=8)
    for fetch in fetches[1:4]:
        fetch.wait()
    pl.semaphore_wait(barrier, n)

    for b in halvings(0):
        for k in (0, 1):
            z_push(0, b, k)
    for k in (0, 1):
        x_push(0, k)
        c_push(0, 0, k)
    low_bits, len_bits = cols.bit_length() - 1, length.bit_length() - 1
    wide = lax.broadcasted_iota(jnp.int32, (length, length), 1)
    tall = lax.broadcasted_iota(jnp.int32, (length, length), 0)

    def upright(ref):
        return jnp.sum(jnp.where(wide == tall, ref[...].astype(jnp.float32), 0.0), axis=1, keepdims=True)

    def slots(shape, axis):
        t = lax.broadcasted_iota(jnp.int32, shape, axis)
        return [t >> low_bits, me * cols + (t & (cols - 1)), me * rows_here + (t >> len_bits), t & (length - 1)]

    def fields(axis):
        shape = (tokens, length) if axis == 0 else (length, tokens)
        lists = (row_ref, col_ref, row_ref, col_ref)
        which = lax.broadcasted_iota(jnp.int32, shape, 1 - axis)
        out = []
        for ref, slot in zip(lists, slots(shape, axis)):
            values = ref[...].astype(jnp.float32) if axis == 0 else upright(ref)
            picked = jnp.where(which == slot, values, 0.0)
            out.append(jnp.sum(picked, axis=1 - axis, keepdims=True).astype(jnp.int32))
        return out

    for k, value in enumerate(fields(0)):
        mc_ref[:, k + 1 : k + 2] = value
    for k, value in enumerate(fields(1)):
        mr_ref[k + 1 : k + 2, :] = value

    def project(source, first):
        normed = rms_scale(source[...].reshape(tokens, width), gain_a_ref[...]).astype(jnp.bfloat16)
        for buf, base, factor in ((q_buf, 0, scale), (k_buf, width, None), (v_buf, 2 * width, None)):
            made = dot(normed, w_qkv_ref[:, base + first : base + first + split]).astype(jnp.bfloat16)
            buf[...] = made if factor is None else made * jnp.bfloat16(factor)

    def attend(write, marks, level, along_ell):
        def body(i, carry):
            rows = pl.ds(pl.multiple_of(i * step, step), step)
            ell_q, col_q = mc_ref[rows, level : level + 1], mc_ref[rows, marks : marks + 1]
            ell_k, col_k = mr_ref[level : level + 1, :], mr_ref[marks : marks + 1, :]
            if along_ell:
                same, diff = col_q == col_k, ell_k - ell_q
            else:
                same, diff = ell_q == ell_k, col_k - col_q
            allowed = same & (diff >= -(WIN // 2)) & (diff < WIN // 2) & (ell_k >= col_k)
            for p in range(split // pair):
                lanes = slice(p * pair, (p + 1) * pair)
                write(i, rows, lanes, attention(q_buf[rows, lanes], k_buf[:, lanes], v_buf[:, lanes], allowed, pair))
            return carry

        lax.fori_loop(0, tokens // step, body, 0)

    def write_ell(i, rows, lanes, value):
        slabs = step // cols
        ell_out[pl.ds(i * slabs, slabs), :, lanes] = value.reshape(slabs, cols, pair).astype(jnp.bfloat16)

    def write_m(i, rows, lanes, value):
        attn_m[rows, lanes] = value.astype(jnp.bfloat16)

    every = sorted(range(1, outer), key=lambda d: (bin(d).count("1"), -d))
    early = [d for d in every if bin(d).count("1") == 1]
    late = every[len(early):]
    fetches[4].wait()
    project(sent, 0)
    attend(write_ell, 2, 1, True)
    for d in early[:-1]:
        on_z(d, 0)
        on_z(d, 1)
    on_z(1, 0)
    on_z(1, 1)
    on_x(0, 0)
    on_x(0, 1)
    for d in late:
        on_z(d, 0)
        on_z(d, 1)
    tokens_out(sent, got, sx_send, sx_recv)
    tokens_out(ell_out, got_ell, sa_send, sa_recv)
    if x_half(0) is not None:
        on_y(1, 0, 0)
        on_y(1, 0, 1)
    for d in early[:-1]:
        on_x(d, 0)
        on_x(d, 1)
    on_x(1, 0)
    on_x(1, 1)
    for d in early[:-1]:
        on_y(0, d, 0)
        on_y(0, d, 1)
    for d in late:
        on_x(d, 0)
        on_x(d, 1)
    for d in early[:-1]:
        on_y(1, d, 0)
        on_y(1, d, 1)
    for d in late:
        on_y(0, d, 0)
        on_y(0, d, 1)
    tokens_in(sent, got, sx_send, sx_recv)
    project(got, split)
    attend(write_m, 4, 3, False)
    tokens_in(ell_out, got_ell, sa_send, sa_recv)
    fetches[5].wait()
    resid = got[...].reshape(tokens, width).astype(jnp.float32) + (
        dot(got_ell[...].reshape(tokens, split), w_out_ref[:split, :]) + dot(attn_m[...], w_out_ref[split:, :])
    )
    normed_ffn = rms_scale(resid, gain_f_ref[...]).astype(jnp.bfloat16)
    if x_half(1) is not None:
        on_y(1, 1, 0)
        on_y(1, 1, 1)
    for d in late:
        on_y(1, d, 0)
        on_y(1, d, 1)
    on_core(0)
    gate = dot(normed_ffn, gu[0])
    up = dot(normed_ffn, gu[1])
    hidden = (gate / (1.0 + jnp.exp(-gate)) * up).astype(jnp.bfloat16)
    on_core(1)
    final = resid + dot(hidden, dn[...])
    valid = mc_ref[:, 4:5] <= mc_ref[:, 3:4]
    out_ref[...] = jnp.where(valid, final, 0.0).astype(jnp.bfloat16)
    for made in pending:
        made().wait_send()


def per_device(n, inputs, col_list, row_list, gain_attn, w_qkv, w_out, gain_ffn, w_gate, w_up, w_down):
    length, cols, width = inputs.shape
    rows_here = length // n
    tokens = length * cols
    split = width // 2
    bf16 = jnp.bfloat16
    depth, ff = w_gate.shape
    deep = w_down.shape[0]
    outer = n // 4
    vmem = pl.BlockSpec(memory_space=pltpu.VMEM)
    smem = pl.BlockSpec(memory_space=pltpu.SMEM)
    hbm = pl.BlockSpec(memory_space=pltpu.HBM)
    dma = pltpu.SemaphoreType.DMA
    result = pl.pallas_call(
        functools.partial(kernel, n),
        out_shape=pltpu.VMEM((tokens, width), bf16),
        in_specs=[hbm, smem, vmem, vmem, vmem, hbm, hbm, vmem, hbm, hbm, hbm],
        out_specs=vmem,
        scratch_shapes=[
            pltpu.VMEM(w_qkv.shape, bf16),
            pltpu.VMEM(w_out.shape, bf16),
            dma((6,)),
            pltpu.VMEM((tokens, 8), jnp.int32),
            pltpu.VMEM((8, tokens), jnp.int32),
            pltpu.VMEM((length, cols, width), bf16),
            pltpu.VMEM((length, cols, width), bf16),
            pltpu.VMEM((length, cols, split), bf16),
            pltpu.VMEM((tokens, split), bf16),
            pltpu.VMEM((tokens, split), bf16),
            pltpu.VMEM((tokens, split), bf16),
            pltpu.VMEM((rows_here, n, cols, width), bf16),
            pltpu.VMEM((rows_here, n, cols, split), bf16),
            pltpu.VMEM((tokens, split), bf16),
            pltpu.VMEM((2, depth * n, ff), bf16),
            pltpu.VMEM((deep * n, width), bf16),
            dma((n,)), dma((n,)), dma((n,)), dma((n,)),
            dma((outer, 2)), dma((outer, 2)),
            dma((outer, 2)), dma((outer, 2)),
            dma((2 * outer, 2)), dma((2 * outer, 2)),
            dma((4 * outer, 2)), dma((4 * outer, 2)),
        ],
        compiler_params=pltpu.CompilerParams(
            collective_id=0, has_side_effects=True, vmem_limit_bytes=VMEM_MIB * 1024 * 1024
        ),
    )(
        *(
            pltpu.with_memory_space_constraint(a, space)
            for a, space in zip(
                (
                    inputs, row_list, col_list.reshape(1, length), row_list.reshape(1, length), gain_attn.reshape(1, width),
                    w_qkv, w_out, gain_ffn.reshape(1, width), w_gate, w_up, w_down,
                ),
                (pltpu.HBM,) * 11,
            )
        )
    )
    return result.reshape(rows_here, length, width)


def solution(mesh):
    placed = (
        P("sample", "harm", None),
        P("sample"),
        P("sample"),
        P(),
        P(),
        P(),
        P(),
        P("harm", None),
        P("harm", None),
        P("harm", None),
    )
    return jax.shard_map(
        functools.partial(per_device, mesh.shape["harm"]),
        mesh=mesh, in_specs=placed, out_specs=P("harm", "sample", None), check_vma=False,
    )
```

```python
import functools

import jax
import jax.numpy as jnp
from jax import lax
from jax.experimental import pallas as pl
from jax.experimental.pallas import tpu as pltpu
from jax.sharding import PartitionSpec as P

HEADS = 8
WIN = 256
VMEM_MIB = 40
MESH = pl.DeviceIdType.MESH

eps = 1e-06
masked = -1e30


def rms_scale(values, gain):
    values = values.astype(jnp.float32)
    mean_sq = jnp.mean(values * values, axis=-1, keepdims=True)
    return values * lax.rsqrt(mean_sq + eps) * gain


def dot(a, b):
    return jnp.dot(a, b, preferred_element_type=jnp.float32)


def attention(query, keys, values, allowed, pair):
    low = lax.broadcasted_iota(jnp.int32, query.shape, 1) < pair // 2
    zero = jnp.zeros_like(query)
    mixed = []
    for part in (jnp.where(low, query, zero), jnp.where(low, zero, query)):
        scores = lax.dot_general(part, keys, (((1,), (1,)), ((), ())), preferred_element_type=jnp.float32)
        scores = jnp.where(allowed, scores, masked)
        top = jnp.max(scores, axis=-1, keepdims=True)
        weights = jnp.exp(scores - top)
        total = jnp.sum(weights, axis=-1, keepdims=True)
        mixed.append(dot(weights.astype(jnp.bfloat16), values) * (1.0 / total))
    return jnp.where(low, mixed[0], mixed[1])


def low_bit(d):
    return d & -d


def kernel(
    n, x_hbm, rows_smem, col_ref, row_ref, gain_a_ref, w_qkv_hbm, w_out_hbm, gain_f_ref, gate_hbm, up_hbm, down_hbm,
    out_ref, w_qkv_ref, w_out_ref, l_sem, mc_ref, mr_ref, x_ref, sent, ell_out, q_buf, k_buf, v_buf, got, got_ell, attn_m, gu, dn,
    sx_send, sx_recv, sa_send, sa_recv, z_send, z_recv, x_send, x_recv, y_send, y_recv, c_send, c_recv, known,
):
    me = lax.axis_index("harm")
    sample = lax.axis_index("sample")
    part = sample % 2
    other_plane = {"sample": sample + 1 - 2 * part, "harm": me}
    outer = n // 4
    zc, inner = me // 4, me % 4
    side, core = inner // 2, inner % 2
    other_side = {"harm": zc * 4 + (1 - side) * 2 + core}
    other_core = {"harm": zc * 4 + side * 2 + (1 - core)}
    depth = gate_hbm.shape[0]
    deep = down_hbm.shape[0]
    length, cols, width = x_ref.shape
    rows_here = length // n
    tokens = length * cols
    split = width // 2
    head_dim = width // HEADS
    pair = 2 * head_dim
    scale = head_dim ** (-0.5)
    step = min(tokens, 256)

    own_gu = pl.ds(pl.multiple_of(me * depth, depth), depth)
    own_dn = pl.ds(pl.multiple_of(me * deep, deep), deep)
    fetches = [
        pltpu.make_async_copy(a, b, l_sem.at[k])
        for k, (a, b) in enumerate((
            (x_hbm, x_ref), (gate_hbm, gu.at[0, own_gu, :]), (up_hbm, gu.at[1, own_gu, :]), (down_hbm, dn.at[own_dn, :]),
            (w_qkv_hbm, w_qkv_ref), (w_out_hbm, w_out_ref),
        ))
    ]
    for fetch in fetches:
        fetch.start()

    bits = [1 << i for i in reversed(range(outer.bit_length() - 1))]

    def across(z, d):
        for b in bits:
            if d & b:
                z = z + b * (1 - 2 * ((z // b) % 2))
        return z

    cube = [{"harm": across(zc, b) * 4 + inner} for b in bits] + [other_side, other_core]
    barrier = pltpu.get_barrier_semaphore()
    for device in cube + [other_plane]:
        pl.semaphore_signal(barrier, inc=1, device_id=device, device_id_type=MESH)

    def tell(r):
        for device in cube:
            pl.semaphore_signal(known.at[r], inc=1, device_id=device, device_id_type=MESH)

    def hear(r):
        pl.semaphore_wait(known.at[r], len(cube))

    rounds = len(cube) - 1

    def place(z, s, c):
        return z * 4 + s * 2 + c

    def piece(k, i, half):
        size = (depth, deep)[k]
        first, rows = i * size, size
        if half is not None:
            rows = size // 2
            first = first + half * rows
        where = pl.ds(pl.multiple_of(first, rows), rows)
        return gu.at[:, where, :] if k == 0 else dn.at[where, :]

    pending = []

    def copy_of(k, i, half, send, recv, slot, device):
        view = piece(k, i, half)
        return pltpu.make_async_remote_copy(
            src_ref=view, dst_ref=view, send_sem=send.at[slot, k], recv_sem=recv.at[slot, k],
            device_id=device, device_id_type=MESH,
        )

    def push(*args):
        copy_of(*args).start()
        pending.append(lambda: copy_of(*args))

    def own_push(k, half, send, recv, slot, device):
        args = (k, me, half, send, recv, slot, device)
        rows = (depth, deep)[k]
        held = pl.ds(0, rows) if half is None else pl.ds(pl.multiple_of(half * (rows // 2), rows // 2), rows // 2)
        for ref, to in ((gate_hbm, piece(0, me, half).at[0]), (up_hbm, piece(0, me, half).at[1])) if k == 0 else ((down_hbm, piece(1, me, half)),):
            pltpu.make_async_remote_copy(
                src_ref=ref.at[held, :], dst_ref=to, send_sem=send.at[slot, k], recv_sem=recv.at[slot, k],
                device_id=device, device_id_type=MESH,
            ).start()
        pending.append(lambda: copy_of(*args))

    def z_half(d):
        return None if d == 0 else part

    def x_half(d):
        return None if d == 0 else part

    def z_push(d, b, k):
        device = {"harm": across(zc, b) * 4 + inner}
        push(k, place(across(zc, d), side, core), z_half(d | b), z_send, z_recv, d | b, device)

    def x_push(d, k):
        push(k, place(across(zc, d), side, core), x_half(d), x_send, x_recv, d, other_side)

    def y_push(other, d, k):
        s = 1 - side if other else side
        push(k, place(across(zc, d), s, core), part, y_send, y_recv, other * outer + d, other_plane)

    def c_args(kind, d, k, c):
        s = 1 - side if kind % 2 else side
        half = (z_half(d), x_half(d))[kind] if kind < 2 else 1 - part
        return k, place(across(zc, d), s, c), half, c_send, c_recv, kind * outer + d, other_core

    def c_push(kind, d, k):
        push(*c_args(kind, d, k, core))

    def halvings(d):
        top = outer if d == 0 else low_bit(d)
        return [b for b in bits if b < top]

    def on_z(d, k):
        copy_of(k, place(across(zc, d), side, core), z_half(d), z_send, z_recv, d, other_core).wait_recv()
        for b in halvings(d):
            z_push(d, b, k)
        x_push(d, k)
        if z_half(d) is not None:
            y_push(0, d, k)
        c_push(0, d, k)

    def on_x(d, k):
        half = x_half(d)
        copy_of(k, place(across(zc, d), 1 - side, core), half, x_send, x_recv, d, other_side).wait_recv()
        if half is not None:
            y_push(1, d, k)
        c_push(1, d, k)

    def on_y(other, d, k):
        s = 1 - side if other else side
        slot = other * outer + d
        copy_of(k, place(across(zc, d), s, core), 1 - part, y_send, y_recv, slot, other_plane).wait_recv()
        c_push(2 + other, d, k)

    def on_core(k):
        for d in range(outer):
            for kind in range(4):
                if kind == 2 and z_half(d) is None or kind == 3 and x_half(d) is None:
                    continue
                copy_of(*c_args(kind, d, k, 1 - core)).wait_recv()

    def to_row(src, dst, send, recv, d):
        peer = (me + d) % n
        return pltpu.make_async_remote_copy(
            src_ref=src.at[pl.ds(peer * rows_here, rows_here)], dst_ref=dst.at[:, me],
            send_sem=send.at[d], recv_sem=recv.at[d], device_id={"harm": peer}, device_id_type=MESH,
        )

    def tokens_out(src, dst, send, recv):
        for d in range(1, n):
            to_row(src, dst, send, recv, d).start()
            pending.append(lambda d=d: to_row(src, dst, send, recv, d))
        dst[:, me] = src[pl.ds(me * rows_here, rows_here)]

    def tokens_in(src, dst, send, recv):
        for d in range(1, n):
            to_row(src, dst, send, recv, d).wait_recv()

    pl.semaphore_wait(barrier, len(cube) + 1)
    for b in halvings(0):
        device = {"harm": across(zc, b) * 4 + inner}
        for k in (0, 1):
            own_push(k, z_half(b), z_send, z_recv, b, device)
    for k in (0, 1):
        own_push(k, x_half(0), x_send, x_recv, 0, other_side)
        own_push(k, None, c_send, c_recv, 0, other_core)
    tell(0)

    low_bits, len_bits = cols.bit_length() - 1, length.bit_length() - 1
    wide = lax.broadcasted_iota(jnp.int32, (length, length), 1)
    tall = lax.broadcasted_iota(jnp.int32, (length, length), 0)

    def upright(ref):
        return jnp.sum(jnp.where(wide == tall, ref[...].astype(jnp.float32), 0.0), axis=1, keepdims=True)

    def slots(shape, axis):
        t = lax.broadcasted_iota(jnp.int32, shape, axis)
        return [t >> low_bits, me * cols + (t & (cols - 1)), me * rows_here + (t >> len_bits), t & (length - 1)]

    def fields(axis):
        shape = (tokens, length) if axis == 0 else (length, tokens)
        lists = (row_ref, col_ref, row_ref, col_ref)
        which = lax.broadcasted_iota(jnp.int32, shape, 1 - axis)
        out = []
        for ref, slot in zip(lists, slots(shape, axis)):
            values = ref[...].astype(jnp.float32) if axis == 0 else upright(ref)
            picked = jnp.where(which == slot, values, 0.0)
            out.append(jnp.sum(picked, axis=1 - axis, keepdims=True).astype(jnp.int32))
        return out

    for k, value in enumerate(fields(0)):
        mc_ref[:, k + 1 : k + 2] = value
    for k, value in enumerate(fields(1)):
        mr_ref[k + 1 : k + 2, :] = value

    def project(source, first):
        normed = rms_scale(source[...].reshape(tokens, width), gain_a_ref[...]).astype(jnp.bfloat16)
        for buf, base, factor in ((q_buf, 0, scale), (k_buf, width, None), (v_buf, 2 * width, None)):
            made = dot(normed, w_qkv_ref[:, base + first : base + first + split]).astype(jnp.bfloat16)
            buf[...] = made if factor is None else made * jnp.bfloat16(factor)

    def attend(write, marks, level, along_ell):
        def body(i, carry):
            rows = pl.ds(pl.multiple_of(i * step, step), step)
            ell_q, col_q = mc_ref[rows, level : level + 1], mc_ref[rows, marks : marks + 1]
            ell_k, col_k = mr_ref[level : level + 1, :], mr_ref[marks : marks + 1, :]
            if along_ell:
                same, diff = col_q == col_k, ell_k - ell_q
            else:
                same, diff = ell_q == ell_k, col_k - col_q
            allowed = same & (diff >= -(WIN // 2)) & (diff < WIN // 2) & (ell_k >= col_k)
            for p in range(split // pair):
                lanes = slice(p * pair, (p + 1) * pair)
                write(i, rows, lanes, attention(q_buf[rows, lanes], k_buf[:, lanes], v_buf[:, lanes], allowed, pair))
            return carry

        lax.fori_loop(0, tokens // step, body, 0)

    def write_ell(i, rows, lanes, value):
        slabs = step // cols
        ell_out[pl.ds(i * slabs, slabs), :, lanes] = value.reshape(slabs, cols, pair).astype(jnp.bfloat16)

    def write_m(i, rows, lanes, value):
        attn_m[rows, lanes] = value.astype(jnp.bfloat16)

    every = sorted(range(1, outer), key=lambda d: (bin(d).count("1"), -d))
    early = [d for d in every if bin(d).count("1") == 1]
    late = every[len(early):]
    fetches[0].wait()

    def order(slot, carry):
        sent[slot] = x_ref[rows_smem[slot]]
        return carry

    lax.fori_loop(0, length, order, 0, unroll=8)
    for fetch in fetches[1:4]:
        fetch.wait()
    fetches[4].wait()
    project(sent, 0)
    hear(0)
    tell(1)
    attend(write_ell, 2, 1, True)
    every = sorted(range(1, outer), key=lambda d: (bin(d).count("1"), -d))
    early = [d for d in every if bin(d).count("1") == 1]
    late = every[len(early):]
    on_z(1, 0)
    on_z(1, 1)
    hear(1)
    tell(2)
    for d in early[:-1]:
        on_z(d, 0)
        on_z(d, 1)
    on_x(0, 0)
    on_x(0, 1)
    on_x(1, 0)
    on_x(1, 1)
    for r in range(2, rounds):
        hear(r)
        if r + 1 < rounds:
            tell(r + 1)
    for d in late:
        on_z(d, 0)
        on_z(d, 1)
    if z_half(1) is not None:
        on_y(0, 1, 0)
        on_y(0, 1, 1)
    tokens_out(sent, got, sx_send, sx_recv)
    tokens_out(ell_out, got_ell, sa_send, sa_recv)
    for d in early[:-1]:
        on_x(d, 0)
        on_x(d, 1)
    for d in early[:-1]:
        on_y(0, d, 0)
        on_y(0, d, 1)
    for d in late:
        on_x(d, 0)
        on_x(d, 1)
    if x_half(1) is not None:
        on_y(1, 1, 0)
        on_y(1, 1, 1)
    for d in early[:-1]:
        on_y(1, d, 0)
        on_y(1, d, 1)
    tokens_in(sent, got, sx_send, sx_recv)
    project(got, split)
    for d in late:
        on_y(0, d, 0)
        on_y(0, d, 1)
    attend(write_m, 4, 3, False)
    tokens_in(ell_out, got_ell, sa_send, sa_recv)
    fetches[5].wait()
    resid = got[...].reshape(tokens, width).astype(jnp.float32) + (
        dot(got_ell[...].reshape(tokens, split), w_out_ref[:split, :]) + dot(attn_m[...], w_out_ref[split:, :])
    )
    normed_ffn = rms_scale(resid, gain_f_ref[...]).astype(jnp.bfloat16)
    for d in late:
        on_y(1, d, 0)
        on_y(1, d, 1)
    on_core(0)
    gate = dot(normed_ffn, gu[0])
    up = dot(normed_ffn, gu[1])
    hidden = (gate / (1.0 + jnp.exp(-gate)) * up).astype(jnp.bfloat16)
    on_core(1)
    final = resid + dot(hidden, dn[...])
    valid = mc_ref[:, 4:5] <= mc_ref[:, 3:4]
    out_ref[...] = jnp.where(valid, final, 0.0).astype(jnp.bfloat16)
    for made in pending:
        made().wait_send()


def per_device(n, inputs, col_list, row_list, gain_attn, w_qkv, w_out, gain_ffn, w_gate, w_up, w_down):
    length, cols, width = inputs.shape
    rows_here = length // n
    tokens = length * cols
    split = width // 2
    bf16 = jnp.bfloat16
    depth, ff = w_gate.shape
    deep = w_down.shape[0]
    outer = n // 4
    vmem = pl.BlockSpec(memory_space=pltpu.VMEM)
    smem = pl.BlockSpec(memory_space=pltpu.SMEM)
    hbm = pl.BlockSpec(memory_space=pltpu.HBM)
    dma = pltpu.SemaphoreType.DMA
    result = pl.pallas_call(
        functools.partial(kernel, n),
        out_shape=pltpu.VMEM((tokens, width), bf16),
        in_specs=[hbm, smem, vmem, vmem, vmem, hbm, hbm, vmem, hbm, hbm, hbm],
        out_specs=vmem,
        scratch_shapes=[
            pltpu.VMEM(w_qkv.shape, bf16),
            pltpu.VMEM(w_out.shape, bf16),
            dma((6,)),
            pltpu.VMEM((tokens, 8), jnp.int32),
            pltpu.VMEM((8, tokens), jnp.int32),
            pltpu.VMEM((length, cols, width), bf16),
            pltpu.VMEM((length, cols, width), bf16),
            pltpu.VMEM((length, cols, split), bf16),
            pltpu.VMEM((tokens, split), bf16),
            pltpu.VMEM((tokens, split), bf16),
            pltpu.VMEM((tokens, split), bf16),
            pltpu.VMEM((rows_here, n, cols, width), bf16),
            pltpu.VMEM((rows_here, n, cols, split), bf16),
            pltpu.VMEM((tokens, split), bf16),
            pltpu.VMEM((2, depth * n, ff), bf16),
            pltpu.VMEM((deep * n, width), bf16),
            dma((n,)), dma((n,)), dma((n,)), dma((n,)),
            dma((outer, 2)), dma((outer, 2)),
            dma((outer, 2)), dma((outer, 2)),
            dma((2 * outer, 2)), dma((2 * outer, 2)),
            dma((4 * outer, 2)), dma((4 * outer, 2)),
            pltpu.SemaphoreType.REGULAR((n.bit_length(),)),
        ],
        compiler_params=pltpu.CompilerParams(
            collective_id=0, has_side_effects=True, vmem_limit_bytes=VMEM_MIB * 1024 * 1024
        ),
    )(
        *(
            pltpu.with_memory_space_constraint(a, space)
            for a, space in zip(
                (
                    inputs, row_list, col_list.reshape(1, length), row_list.reshape(1, length), gain_attn.reshape(1, width),
                    w_qkv, w_out, gain_ffn.reshape(1, width), w_gate, w_up, w_down,
                ),
                (pltpu.HBM,) * 11,
            )
        )
    )
    return result.reshape(rows_here, length, width)


def solution(mesh):
    placed = (
        P("sample", "harm", None),
        P("sample"),
        P("sample"),
        P(),
        P(),
        P(),
        P(),
        P("harm", None),
        P("harm", None),
        P("harm", None),
    )
    return jax.shard_map(
        functools.partial(per_device, mesh.shape["harm"]),
        mesh=mesh, in_specs=placed, out_specs=P("harm", "sample", None), check_vma=False,
    )
```

```python
import functools

import jax
import jax.numpy as jnp
from jax import lax
from jax.experimental import pallas as pl
from jax.experimental.pallas import tpu as pltpu
from jax.sharding import PartitionSpec as P

HEADS = 8
WIN = 256
VMEM_MIB = 40
MESH = pl.DeviceIdType.MESH

eps = 1e-06
masked = -1e30


def rms_scale(values, gain):
    values = values.astype(jnp.float32)
    mean_sq = jnp.mean(values * values, axis=-1, keepdims=True)
    return values * lax.rsqrt(mean_sq + eps) * gain


def dot(a, b):
    return jnp.dot(a, b, preferred_element_type=jnp.float32)


def attention(query, keys, values, allowed, pair):
    low = lax.broadcasted_iota(jnp.int32, query.shape, 1) < pair // 2
    zero = jnp.zeros_like(query)
    mixed = []
    for part in (jnp.where(low, query, zero), jnp.where(low, zero, query)):
        scores = lax.dot_general(part, keys, (((1,), (1,)), ((), ())), preferred_element_type=jnp.float32)
        scores = jnp.where(allowed, scores, masked)
        top = jnp.max(scores, axis=-1, keepdims=True)
        weights = jnp.exp(scores - top)
        total = jnp.sum(weights, axis=-1, keepdims=True)
        mixed.append(dot(weights.astype(jnp.bfloat16), values) * (1.0 / total))
    return jnp.where(low, mixed[0], mixed[1])


def low_bit(d):
    return d & -d


def kernel(
    n, x_hbm, rows_smem, col_ref, row_ref, gain_a_ref, w_qkv_hbm, w_out_hbm, gain_f_ref, gate_hbm, up_hbm, down_hbm,
    out_ref, w_qkv_ref, w_out_ref, l_sem, mc_ref, mr_ref, x_ref, sent, ell_out, q_buf, k_buf, v_buf, got, got_ell, attn_m, gu, dn,
    sx_send, sx_recv, sa_send, sa_recv, z_send, z_recv, x_send, x_recv, y_send, y_recv, c_send, c_recv, known,
):
    me = lax.axis_index("harm")
    sample = lax.axis_index("sample")
    part = sample % 2
    other_plane = {"sample": sample + 1 - 2 * part, "harm": me}
    outer = n // 4
    zc, inner = me // 4, me % 4
    side, core = inner // 2, inner % 2
    other_side = {"harm": zc * 4 + (1 - side) * 2 + core}
    other_core = {"harm": zc * 4 + side * 2 + (1 - core)}
    depth = gate_hbm.shape[0]
    deep = down_hbm.shape[0]
    length, cols, width = x_ref.shape
    rows_here = length // n
    tokens = length * cols
    split = width // 2
    head_dim = width // HEADS
    pair = 2 * head_dim
    scale = head_dim ** (-0.5)
    step = min(tokens, 256)

    own_gu = pl.ds(pl.multiple_of(me * depth, depth), depth)
    own_dn = pl.ds(pl.multiple_of(me * deep, deep), deep)
    fetches = [
        pltpu.make_async_copy(a, b, l_sem.at[k])
        for k, (a, b) in enumerate((
            (x_hbm, x_ref), (gate_hbm, gu.at[0, own_gu, :]), (up_hbm, gu.at[1, own_gu, :]), (down_hbm, dn.at[own_dn, :]),
            (w_qkv_hbm, w_qkv_ref), (w_out_hbm, w_out_ref),
        ))
    ]
    for fetch in fetches:
        fetch.start()

    bits = [1 << i for i in reversed(range(outer.bit_length() - 1))]

    def across(z, d):
        for b in bits:
            if d & b:
                z = z + b * (1 - 2 * ((z // b) % 2))
        return z

    cube = [{"harm": across(zc, b) * 4 + inner} for b in bits] + [other_side, other_core]
    barrier = pltpu.get_barrier_semaphore()
    for device in cube + [other_plane]:
        pl.semaphore_signal(barrier, inc=1, device_id=device, device_id_type=MESH)

    def tell(r):
        for device in cube:
            pl.semaphore_signal(known.at[r], inc=1, device_id=device, device_id_type=MESH)

    def hear(r):
        pl.semaphore_wait(known.at[r], len(cube))

    rounds = len(cube) - 1

    def place(z, s, c):
        return z * 4 + s * 2 + c

    def piece(k, i, half):
        size = (depth, deep)[k]
        first, rows = i * size, size
        if half is not None:
            rows = size // 2
            first = first + half * rows
        where = pl.ds(pl.multiple_of(first, rows), rows)
        return gu.at[:, where, :] if k == 0 else dn.at[where, :]

    pending = []

    def copy_of(k, i, half, send, recv, slot, device):
        view = piece(k, i, half)
        return pltpu.make_async_remote_copy(
            src_ref=view, dst_ref=view, send_sem=send.at[slot, k], recv_sem=recv.at[slot, k],
            device_id=device, device_id_type=MESH,
        )

    def push(*args):
        copy_of(*args).start()
        pending.append(lambda: copy_of(*args))

    def own_push(k, half, send, recv, slot, device):
        args = (k, me, half, send, recv, slot, device)
        rows = (depth, deep)[k]
        held = pl.ds(0, rows) if half is None else pl.ds(pl.multiple_of(half * (rows // 2), rows // 2), rows // 2)
        for ref, to in ((gate_hbm, piece(0, me, half).at[0]), (up_hbm, piece(0, me, half).at[1])) if k == 0 else ((down_hbm, piece(1, me, half)),):
            pltpu.make_async_remote_copy(
                src_ref=ref.at[held, :], dst_ref=to, send_sem=send.at[slot, k], recv_sem=recv.at[slot, k],
                device_id=device, device_id_type=MESH,
            ).start()
        pending.append(lambda: copy_of(*args))

    def z_half(d):
        return None if d == 0 else part

    def x_half(d):
        return None if d == 0 else part

    def z_push(d, b, k):
        device = {"harm": across(zc, b) * 4 + inner}
        push(k, place(across(zc, d), side, core), z_half(d | b), z_send, z_recv, d | b, device)

    def x_push(d, k):
        push(k, place(across(zc, d), side, core), x_half(d), x_send, x_recv, d, other_side)

    def y_push(other, d, k):
        s = 1 - side if other else side
        push(k, place(across(zc, d), s, core), part, y_send, y_recv, other * outer + d, other_plane)

    def c_args(other, d, k, c):
        s = 1 - side if other else side
        return k, place(across(zc, d), s, c), None, c_send, c_recv, other * outer + d, other_core

    def c_push(other, d, k):
        push(*c_args(other, d, k, core))

    def halvings(d):
        top = outer if d == 0 else low_bit(d)
        return [b for b in bits if b < top]

    def on_z(d, k):
        copy_of(k, place(across(zc, d), side, core), z_half(d), z_send, z_recv, d, other_core).wait_recv()
        for b in halvings(d):
            z_push(d, b, k)
        x_push(d, k)
        y_push(0, d, k)

    def on_x(d, k):
        half = x_half(d)
        copy_of(k, place(across(zc, d), 1 - side, core), half, x_send, x_recv, d, other_side).wait_recv()
        if half is not None:
            y_push(1, d, k)
        else:
            c_push(1, d, k)

    def on_y(other, d, k):
        s = 1 - side if other else side
        slot = other * outer + d
        copy_of(k, place(across(zc, d), s, core), 1 - part, y_send, y_recv, slot, other_plane).wait_recv()
        c_push(other, d, k)

    def on_core(k):
        for d in range(outer):
            for other in (0, 1):
                copy_of(*c_args(other, d, k, 1 - core)).wait_recv()

    def to_row(src, dst, send, recv, d):
        peer = (me + d) % n
        return pltpu.make_async_remote_copy(
            src_ref=src.at[pl.ds(peer * rows_here, rows_here)], dst_ref=dst.at[:, me],
            send_sem=send.at[0], recv_sem=recv.at[0], device_id={"harm": peer}, device_id_type=MESH,
        )

    def tokens_out(src, dst, send, recv):
        for d in range(1, n):
            to_row(src, dst, send, recv, d).start()
        dst[:, me] = src[pl.ds(me * rows_here, rows_here)]

    def all_rows(src, dst, send, recv):
        return pltpu.make_async_remote_copy(
            src_ref=src.at[pl.ds(0, rows_here * (n - 1))], dst_ref=dst.at[:, pl.ds(0, n - 1)],
            send_sem=send.at[0], recv_sem=recv.at[0], device_id=other_core, device_id_type=MESH,
        )

    def tokens_in(src, dst, send, recv):
        all_rows(src, dst, send, recv).wait_recv()

    pl.semaphore_wait(barrier, len(cube) + 1)
    for b in halvings(0):
        device = {"harm": across(zc, b) * 4 + inner}
        for k in (0, 1):
            own_push(k, z_half(b), z_send, z_recv, b, device)
    for k in (0, 1):
        own_push(k, x_half(0), x_send, x_recv, 0, other_side)
        own_push(k, None, c_send, c_recv, 0, other_core)
    tell(0)

    low_bits, len_bits = cols.bit_length() - 1, length.bit_length() - 1
    wide = lax.broadcasted_iota(jnp.int32, (length, length), 1)
    tall = lax.broadcasted_iota(jnp.int32, (length, length), 0)

    def upright(ref):
        return jnp.sum(jnp.where(wide == tall, ref[...].astype(jnp.float32), 0.0), axis=1, keepdims=True)

    def slots(shape, axis):
        t = lax.broadcasted_iota(jnp.int32, shape, axis)
        return [t >> low_bits, me * cols + (t & (cols - 1)), me * rows_here + (t >> len_bits), t & (length - 1)]

    def fields(axis):
        shape = (tokens, length) if axis == 0 else (length, tokens)
        lists = (row_ref, col_ref, row_ref, col_ref)
        which = lax.broadcasted_iota(jnp.int32, shape, 1 - axis)
        out = []
        for ref, slot in zip(lists, slots(shape, axis)):
            values = ref[...].astype(jnp.float32) if axis == 0 else upright(ref)
            picked = jnp.where(which == slot, values, 0.0)
            out.append(jnp.sum(picked, axis=1 - axis, keepdims=True).astype(jnp.int32))
        return out

    for k, value in enumerate(fields(0)):
        mc_ref[:, k + 1 : k + 2] = value
    for k, value in enumerate(fields(1)):
        mr_ref[k + 1 : k + 2, :] = value

    def project(source, first):
        normed = rms_scale(source[...].reshape(tokens, width), gain_a_ref[...]).astype(jnp.bfloat16)
        for buf, base, factor in ((q_buf, 0, scale), (k_buf, width, None), (v_buf, 2 * width, None)):
            made = dot(normed, w_qkv_ref[:, base + first : base + first + split]).astype(jnp.bfloat16)
            buf[...] = made if factor is None else made * jnp.bfloat16(factor)

    def attend(write, marks, level, along_ell):
        def body(i, carry):
            rows = pl.ds(pl.multiple_of(i * step, step), step)
            ell_q, col_q = mc_ref[rows, level : level + 1], mc_ref[rows, marks : marks + 1]
            ell_k, col_k = mr_ref[level : level + 1, :], mr_ref[marks : marks + 1, :]
            if along_ell:
                same, diff = col_q == col_k, ell_k - ell_q
            else:
                same, diff = ell_q == ell_k, col_k - col_q
            allowed = same & (diff >= -(WIN // 2)) & (diff < WIN // 2) & (ell_k >= col_k)
            for p in range(split // pair):
                lanes = slice(p * pair, (p + 1) * pair)
                write(i, rows, lanes, attention(q_buf[rows, lanes], k_buf[:, lanes], v_buf[:, lanes], allowed, pair))
            return carry

        lax.fori_loop(0, tokens // step, body, 0)

    def write_ell(i, rows, lanes, value):
        slabs = step // cols
        ell_out[pl.ds(i * slabs, slabs), :, lanes] = value.reshape(slabs, cols, pair).astype(jnp.bfloat16)

    def write_m(i, rows, lanes, value):
        attn_m[rows, lanes] = value.astype(jnp.bfloat16)

    every = sorted(range(1, outer), key=lambda d: (bin(d).count("1"), -d))
    early = [d for d in every if bin(d).count("1") == 1]
    late = every[len(early):]
    fetches[0].wait()

    def order(slot, carry):
        sent[slot] = x_ref[rows_smem[slot]]
        return carry

    lax.fori_loop(0, length, order, 0, unroll=8)
    for fetch in fetches[1:4]:
        fetch.wait()
    far = [b for b in bits if b > 1]
    late = sorted((d for d in range(1, outer) if d & (d - 1)), key=lambda d: (bin(d).count("1"), -d))
    groups = {"o": [0], "n": [1], "f": far, "l": late}
    handlers = {"z": on_z, "x": on_x, "y": functools.partial(on_y, 0), "d": functools.partial(on_y, 1)}

    def run(*events):
        for stage, group, k in events:
            for d in groups[group]:
                handlers[stage](d, int(k))

    fetches[4].wait()
    project(sent, 0)
    hear(0)
    tell(1)
    attend(write_ell, 2, 1, True)
    run("zn0", "zn1")
    hear(1)
    tell(2)
    run("zf0", "zf1", "xo0", "xo1", "zl0", "zl1", "xn0", "xn1")
    for r in range(2, rounds):
        hear(r)
        if r + 1 < rounds:
            tell(r + 1)
    tokens_out(sent, got, sx_send, sx_recv)
    tokens_out(ell_out, got_ell, sa_send, sa_recv)
    run("yn0", "yn1", "xf0", "xf1", "yf0", "yf1", "dn0", "dn1", "xl0", "xl1", "df0", "df1")
    tokens_in(sent, got, sx_send, sx_recv)
    project(got, split)
    run("yl0", "yl1")
    attend(write_m, 4, 3, False)
    run("dl0", "dl1")
    tokens_in(ell_out, got_ell, sa_send, sa_recv)
    fetches[5].wait()
    resid = got[...].reshape(tokens, width).astype(jnp.float32) + (
        dot(got_ell[...].reshape(tokens, split), w_out_ref[:split, :]) + dot(attn_m[...], w_out_ref[split:, :])
    )
    normed_ffn = rms_scale(resid, gain_f_ref[...]).astype(jnp.bfloat16)
    on_core(0)
    gate = dot(normed_ffn, gu[0])
    up = dot(normed_ffn, gu[1])
    hidden = (gate / (1.0 + jnp.exp(-gate)) * up).astype(jnp.bfloat16)
    on_core(1)
    final = resid + dot(hidden, dn[...])
    valid = mc_ref[:, 4:5] <= mc_ref[:, 3:4]
    out_ref[...] = jnp.where(valid, final, 0.0).astype(jnp.bfloat16)
    for made in pending:
        made().wait_send()
    all_rows(sent, got, sx_send, sx_recv).wait_send()
    all_rows(ell_out, got_ell, sa_send, sa_recv).wait_send()


def per_device(n, inputs, col_list, row_list, gain_attn, w_qkv, w_out, gain_ffn, w_gate, w_up, w_down):
    length, cols, width = inputs.shape
    rows_here = length // n
    tokens = length * cols
    split = width // 2
    bf16 = jnp.bfloat16
    depth, ff = w_gate.shape
    deep = w_down.shape[0]
    outer = n // 4
    vmem = pl.BlockSpec(memory_space=pltpu.VMEM)
    smem = pl.BlockSpec(memory_space=pltpu.SMEM)
    hbm = pl.BlockSpec(memory_space=pltpu.HBM)
    dma = pltpu.SemaphoreType.DMA
    result = pl.pallas_call(
        functools.partial(kernel, n),
        out_shape=pltpu.VMEM((tokens, width), bf16),
        in_specs=[hbm, smem, vmem, vmem, vmem, hbm, hbm, vmem, hbm, hbm, hbm],
        out_specs=vmem,
        scratch_shapes=[
            pltpu.VMEM(w_qkv.shape, bf16),
            pltpu.VMEM(w_out.shape, bf16),
            dma((6,)),
            pltpu.VMEM((tokens, 8), jnp.int32),
            pltpu.VMEM((8, tokens), jnp.int32),
            pltpu.VMEM((length, cols, width), bf16),
            pltpu.VMEM((length, cols, width), bf16),
            pltpu.VMEM((length, cols, split), bf16),
            pltpu.VMEM((tokens, split), bf16),
            pltpu.VMEM((tokens, split), bf16),
            pltpu.VMEM((tokens, split), bf16),
            pltpu.VMEM((rows_here, n, cols, width), bf16),
            pltpu.VMEM((rows_here, n, cols, split), bf16),
            pltpu.VMEM((tokens, split), bf16),
            pltpu.VMEM((2, depth * n, ff), bf16),
            pltpu.VMEM((deep * n, width), bf16),
            dma((1,)), dma((1,)), dma((1,)), dma((1,)),
            dma((outer, 2)), dma((outer, 2)),
            dma((outer, 2)), dma((outer, 2)),
            dma((2 * outer, 2)), dma((2 * outer, 2)),
            dma((2 * outer, 2)), dma((2 * outer, 2)),
            pltpu.SemaphoreType.REGULAR((n.bit_length(),)),
        ],
        compiler_params=pltpu.CompilerParams(
            collective_id=0, has_side_effects=True, vmem_limit_bytes=VMEM_MIB * 1024 * 1024
        ),
    )(
        *(
            pltpu.with_memory_space_constraint(a, space)
            for a, space in zip(
                (
                    inputs, row_list, col_list.reshape(1, length), row_list.reshape(1, length), gain_attn.reshape(1, width),
                    w_qkv, w_out, gain_ffn.reshape(1, width), w_gate, w_up, w_down,
                ),
                (pltpu.HBM,) * 11,
            )
        )
    )
    return result.reshape(rows_here, length, width)


def solution(mesh):
    placed = (
        P("sample", "harm", None),
        P("sample"),
        P("sample"),
        P(),
        P(),
        P(),
        P(),
        P("harm", None),
        P("harm", None),
        P("harm", None),
    )
    return jax.shard_map(
        functools.partial(per_device, mesh.shape["harm"]),
        mesh=mesh, in_specs=placed, out_specs=P("harm", "sample", None), check_vma=False,
    )
```

```python
import functools

import jax
import jax.numpy as jnp
from jax import lax
from jax.experimental import pallas as pl
from jax.experimental.pallas import tpu as pltpu
from jax.sharding import PartitionSpec as P

HEADS = 8
WIN = 256
VMEM_MIB = 40
MESH = pl.DeviceIdType.MESH

eps = 1e-06
masked = -1e30


def rms_scale(values, gain):
    values = values.astype(jnp.float32)
    mean_sq = jnp.mean(values * values, axis=-1, keepdims=True)
    return values * lax.rsqrt(mean_sq + eps) * gain


def dot(a, b):
    return jnp.dot(a, b, preferred_element_type=jnp.float32)


def attention(query, keys, values, allowed, pair):
    low = lax.broadcasted_iota(jnp.int32, query.shape, 1) < pair // 2
    zero = jnp.zeros_like(query)
    mixed = []
    for part in (jnp.where(low, query, zero), jnp.where(low, zero, query)):
        scores = lax.dot_general(part, keys, (((1,), (1,)), ((), ())), preferred_element_type=jnp.float32)
        scores = jnp.where(allowed, scores, masked)
        top = jnp.max(scores, axis=-1, keepdims=True)
        weights = jnp.exp(scores - top)
        total = jnp.sum(weights, axis=-1, keepdims=True)
        mixed.append(dot(weights.astype(jnp.bfloat16), values) * (1.0 / total))
    return jnp.where(low, mixed[0], mixed[1])


def low_bit(d):
    return d & -d


def kernel(
    n, x_hbm, rows_smem, col_ref, row_ref, gain_a_ref, w_qkv_hbm, w_out_hbm, gain_f_ref, gate_hbm, up_hbm, down_hbm,
    out_ref, w_qkv_ref, w_out_ref, l_sem, mc_ref, mr_ref, x_ref, sent, ell_out, q_buf, k_buf, v_buf, got, got_ell, attn_m, gu, dn,
    sx_send, sx_recv, sa_send, sa_recv, z_send, z_recv, x_send, x_recv, y_send, y_recv, c_send, c_recv, known,
):
    me = lax.axis_index("harm")
    sample = lax.axis_index("sample")
    part = sample % 2
    other_plane = {"sample": sample + 1 - 2 * part, "harm": me}
    outer = n // 4
    zc, inner = me // 4, me % 4
    side, core = inner // 2, inner % 2
    other_side = {"harm": zc * 4 + (1 - side) * 2 + core}
    other_core = {"harm": zc * 4 + side * 2 + (1 - core)}
    depth = gate_hbm.shape[0]
    deep = down_hbm.shape[0]
    length, cols, width = x_ref.shape
    rows_here = length // n
    tokens = length * cols
    split = width // 2
    head_dim = width // HEADS
    pair = 2 * head_dim
    scale = head_dim ** (-0.5)
    step = min(tokens, 256)

    own_gu = pl.ds(pl.multiple_of(me * depth, depth), depth)
    own_dn = pl.ds(pl.multiple_of(me * deep, deep), deep)
    fetches = [
        pltpu.make_async_copy(a, b, l_sem.at[k])
        for k, (a, b) in enumerate((
            (x_hbm, x_ref), (gate_hbm, gu.at[0, own_gu, :]), (up_hbm, gu.at[1, own_gu, :]), (down_hbm, dn.at[own_dn, :]),
            (w_qkv_hbm, w_qkv_ref), (w_out_hbm, w_out_ref),
        ))
    ]
    for fetch in fetches:
        fetch.start()

    bits = [1 << i for i in reversed(range(outer.bit_length() - 1))]

    def across(z, d):
        for b in bits:
            if d & b:
                z = z + b * (1 - 2 * ((z // b) % 2))
        return z

    cube = [{"harm": across(zc, b) * 4 + inner} for b in bits] + [other_side, other_core]
    barrier = pltpu.get_barrier_semaphore()
    for device in cube + [other_plane]:
        pl.semaphore_signal(barrier, inc=1, device_id=device, device_id_type=MESH)

    def tell(r):
        for device in cube:
            pl.semaphore_signal(known.at[r], inc=1, device_id=device, device_id_type=MESH)

    def hear(r):
        pl.semaphore_wait(known.at[r], len(cube))

    rounds = len(cube) - 1

    def place(z, s, c):
        return z * 4 + s * 2 + c

    def piece(k, i, half):
        size = (depth, deep)[k]
        first, rows = i * size, size
        if half is not None:
            rows = size // 2
            first = first + half * rows
        where = pl.ds(pl.multiple_of(first, rows), rows)
        return gu.at[:, where, :] if k == 0 else dn.at[where, :]

    pending = []

    def copy_of(k, i, half, send, recv, slot, device):
        view = piece(k, i, half)
        return pltpu.make_async_remote_copy(
            src_ref=view, dst_ref=view, send_sem=send.at[slot, k], recv_sem=recv.at[slot, k],
            device_id=device, device_id_type=MESH,
        )

    def push(*args):
        copy_of(*args).start()
        pending.append(lambda: copy_of(*args))

    def own_push(k, half, send, recv, slot, device):
        args = (k, me, half, send, recv, slot, device)
        rows = (depth, deep)[k]
        held = pl.ds(0, rows) if half is None else pl.ds(pl.multiple_of(half * (rows // 2), rows // 2), rows // 2)
        for ref, to in ((gate_hbm, piece(0, me, half).at[0]), (up_hbm, piece(0, me, half).at[1])) if k == 0 else ((down_hbm, piece(1, me, half)),):
            pltpu.make_async_remote_copy(
                src_ref=ref.at[held, :], dst_ref=to, send_sem=send.at[slot, k], recv_sem=recv.at[slot, k],
                device_id=device, device_id_type=MESH,
            ).start()
        pending.append(lambda: copy_of(*args))

    def z_half(d):
        return None if d == 0 else part

    def x_half(d):
        return None if d == 0 else part

    def z_push(d, b, k):
        device = {"harm": across(zc, b) * 4 + inner}
        push(k, place(across(zc, d), side, core), z_half(d | b), z_send, z_recv, d | b, device)

    def x_push(d, k):
        push(k, place(across(zc, d), side, core), x_half(d), x_send, x_recv, d, other_side)

    def y_push(other, d, k):
        s = 1 - side if other else side
        push(k, place(across(zc, d), s, core), part, y_send, y_recv, other * outer + d, other_plane)

    def c_args(other, d, k, c):
        s = 1 - side if other else side
        return k, place(across(zc, d), s, c), None, c_send, c_recv, other * outer + d, other_core

    def c_push(other, d, k):
        push(*c_args(other, d, k, core))

    def halvings(d):
        top = outer if d == 0 else low_bit(d)
        return [b for b in bits if b < top]

    def on_z(d, k):
        copy_of(k, place(across(zc, d), side, core), z_half(d), z_send, z_recv, d, other_core).wait_recv()
        for b in halvings(d):
            z_push(d, b, k)
        x_push(d, k)
        y_push(0, d, k)

    def on_x(d, k):
        half = x_half(d)
        copy_of(k, place(across(zc, d), 1 - side, core), half, x_send, x_recv, d, other_side).wait_recv()
        if half is not None:
            y_push(1, d, k)
        else:
            c_push(1, d, k)

    def on_y(other, d, k):
        s = 1 - side if other else side
        slot = other * outer + d
        copy_of(k, place(across(zc, d), s, core), 1 - part, y_send, y_recv, slot, other_plane).wait_recv()
        c_push(other, d, k)

    def on_core(k):
        for d in range(outer):
            for other in (0, 1):
                copy_of(*c_args(other, d, k, 1 - core)).wait_recv()

    def to_row(src, dst, send, recv, d):
        peer = (me + d) % n
        return pltpu.make_async_remote_copy(
            src_ref=src.at[pl.ds(peer * rows_here, rows_here)], dst_ref=dst.at[:, me],
            send_sem=send.at[0], recv_sem=recv.at[0], device_id={"harm": peer}, device_id_type=MESH,
        )

    def tokens_out(src, dst, send, recv):
        for d in range(1, n):
            to_row(src, dst, send, recv, d).start()
        dst[:, me] = src[pl.ds(me * rows_here, rows_here)]

    def all_rows(src, dst, send, recv):
        return pltpu.make_async_remote_copy(
            src_ref=src.at[pl.ds(0, rows_here * (n - 1))], dst_ref=dst.at[:, pl.ds(0, n - 1)],
            send_sem=send.at[0], recv_sem=recv.at[0], device_id=other_core, device_id_type=MESH,
        )

    def tokens_in(src, dst, send, recv):
        all_rows(src, dst, send, recv).wait_recv()

    pl.semaphore_wait(barrier, len(cube) + 1)
    for b in halvings(0):
        device = {"harm": across(zc, b) * 4 + inner}
        for k in (0, 1):
            own_push(k, z_half(b), z_send, z_recv, b, device)
    for k in (0, 1):
        own_push(k, x_half(0), x_send, x_recv, 0, other_side)
        own_push(k, None, c_send, c_recv, 0, other_core)
    tell(0)

    low_bits, len_bits = cols.bit_length() - 1, length.bit_length() - 1
    wide = lax.broadcasted_iota(jnp.int32, (length, length), 1)
    tall = lax.broadcasted_iota(jnp.int32, (length, length), 0)

    def upright(ref):
        return jnp.sum(jnp.where(wide == tall, ref[...].astype(jnp.float32), 0.0), axis=1, keepdims=True)

    def slots(shape, axis):
        t = lax.broadcasted_iota(jnp.int32, shape, axis)
        return [t >> low_bits, me * cols + (t & (cols - 1)), me * rows_here + (t >> len_bits), t & (length - 1)]

    def fields(axis):
        shape = (tokens, length) if axis == 0 else (length, tokens)
        lists = (row_ref, col_ref, row_ref, col_ref)
        which = lax.broadcasted_iota(jnp.int32, shape, 1 - axis)
        out = []
        for ref, slot in zip(lists, slots(shape, axis)):
            values = ref[...].astype(jnp.float32) if axis == 0 else upright(ref)
            picked = jnp.where(which == slot, values, 0.0)
            out.append(jnp.sum(picked, axis=1 - axis, keepdims=True).astype(jnp.int32))
        return out

    for k, value in enumerate(fields(0)):
        mc_ref[:, k + 1 : k + 2] = value
    for k, value in enumerate(fields(1)):
        mr_ref[k + 1 : k + 2, :] = value

    def project(source, first):
        normed = rms_scale(source[...].reshape(tokens, width), gain_a_ref[...]).astype(jnp.bfloat16)
        for buf, base, factor in ((q_buf, 0, scale), (k_buf, width, None), (v_buf, 2 * width, None)):
            made = dot(normed, w_qkv_ref[:, base + first : base + first + split]).astype(jnp.bfloat16)
            buf[...] = made if factor is None else made * jnp.bfloat16(factor)

    def attend(write, marks, level, along_ell):
        def body(i, carry):
            rows = pl.ds(pl.multiple_of(i * step, step), step)
            ell_q, col_q = mc_ref[rows, level : level + 1], mc_ref[rows, marks : marks + 1]
            ell_k, col_k = mr_ref[level : level + 1, :], mr_ref[marks : marks + 1, :]
            if along_ell:
                same, diff = col_q == col_k, ell_k - ell_q
            else:
                same, diff = ell_q == ell_k, col_k - col_q
            allowed = same & (diff >= -(WIN // 2)) & (diff < WIN // 2) & (ell_k >= col_k)
            for p in range(split // pair):
                lanes = slice(p * pair, (p + 1) * pair)
                write(i, rows, lanes, attention(q_buf[rows, lanes], k_buf[:, lanes], v_buf[:, lanes], allowed, pair))
            return carry

        lax.fori_loop(0, tokens // step, body, 0)

    def write_ell(i, rows, lanes, value):
        slabs = step // cols
        ell_out[pl.ds(i * slabs, slabs), :, lanes] = value.reshape(slabs, cols, pair).astype(jnp.bfloat16)

    def write_m(i, rows, lanes, value):
        attn_m[rows, lanes] = value.astype(jnp.bfloat16)

    every = sorted(range(1, outer), key=lambda d: (bin(d).count("1"), -d))
    early = [d for d in every if bin(d).count("1") == 1]
    late = every[len(early):]
    fetches[0].wait()

    def order(slot, carry):
        sent[slot] = x_ref[rows_smem[slot]]
        return carry

    lax.fori_loop(0, length, order, 0, unroll=8)
    for fetch in fetches[1:4]:
        fetch.wait()
    far = [b for b in bits if b > 1]
    late = sorted((d for d in range(1, outer) if d & (d - 1)), key=lambda d: (bin(d).count("1"), -d))
    groups = {"o": [0], "n": [1], "f": far, "l": late}
    handlers = {"z": on_z, "x": on_x, "y": functools.partial(on_y, 0), "d": functools.partial(on_y, 1)}

    def run(*events):
        for stage, group, k in events:
            for d in groups[group]:
                handlers[stage](d, int(k))

    fetches[4].wait()
    project(sent, 0)
    hear(0)
    tell(1)
    attend(write_ell, 2, 1, True)
    run("zn0", "zn1")
    hear(1)
    tell(2)
    run("zf0", "zf1", "xo0", "xo1", "zl0", "zl1")
    for r in range(2, rounds):
        hear(r)
        if r + 1 < rounds:
            tell(r + 1)
    tokens_out(sent, got, sx_send, sx_recv)
    run("xn0", "xn1")
    tokens_out(ell_out, got_ell, sa_send, sa_recv)
    run("yn0", "yn1", "xf0", "xf1", "yf0", "yf1", "dn0", "dn1", "xl0", "xl1", "df0", "df1")
    tokens_in(sent, got, sx_send, sx_recv)
    project(got, split)
    run("yl0", "yl1")
    attend(write_m, 4, 3, False)
    run("dl0", "dl1")
    for made in pending[: len(pending) // 2]:
        made().wait_send()
    del pending[: len(pending) // 2]
    tokens_in(ell_out, got_ell, sa_send, sa_recv)
    fetches[5].wait()
    resid = got[...].reshape(tokens, width).astype(jnp.float32) + (
        dot(got_ell[...].reshape(tokens, split), w_out_ref[:split, :]) + dot(attn_m[...], w_out_ref[split:, :])
    )
    normed_ffn = rms_scale(resid, gain_f_ref[...]).astype(jnp.bfloat16)
    on_core(0)
    gate = dot(normed_ffn, gu[0])
    up = dot(normed_ffn, gu[1])
    hidden = (gate / (1.0 + jnp.exp(-gate)) * up).astype(jnp.bfloat16)
    on_core(1)
    final = resid + dot(hidden, dn[...])
    valid = mc_ref[:, 4:5] <= mc_ref[:, 3:4]
    out_ref[...] = jnp.where(valid, final, 0.0).astype(jnp.bfloat16)
    for made in pending:
        made().wait_send()
    all_rows(sent, got, sx_send, sx_recv).wait_send()
    all_rows(ell_out, got_ell, sa_send, sa_recv).wait_send()


def per_device(n, inputs, col_list, row_list, gain_attn, w_qkv, w_out, gain_ffn, w_gate, w_up, w_down):
    length, cols, width = inputs.shape
    rows_here = length // n
    tokens = length * cols
    split = width // 2
    bf16 = jnp.bfloat16
    depth, ff = w_gate.shape
    deep = w_down.shape[0]
    outer = n // 4
    vmem = pl.BlockSpec(memory_space=pltpu.VMEM)
    smem = pl.BlockSpec(memory_space=pltpu.SMEM)
    hbm = pl.BlockSpec(memory_space=pltpu.HBM)
    dma = pltpu.SemaphoreType.DMA
    result = pl.pallas_call(
        functools.partial(kernel, n),
        out_shape=pltpu.VMEM((tokens, width), bf16),
        in_specs=[hbm, smem, vmem, vmem, vmem, hbm, hbm, vmem, hbm, hbm, hbm],
        out_specs=vmem,
        scratch_shapes=[
            pltpu.VMEM(w_qkv.shape, bf16),
            pltpu.VMEM(w_out.shape, bf16),
            dma((6,)),
            pltpu.VMEM((tokens, 8), jnp.int32),
            pltpu.VMEM((8, tokens), jnp.int32),
            pltpu.VMEM((length, cols, width), bf16),
            pltpu.VMEM((length, cols, width), bf16),
            pltpu.VMEM((length, cols, split), bf16),
            pltpu.VMEM((tokens, split), bf16),
            pltpu.VMEM((tokens, split), bf16),
            pltpu.VMEM((tokens, split), bf16),
            pltpu.VMEM((rows_here, n, cols, width), bf16),
            pltpu.VMEM((rows_here, n, cols, split), bf16),
            pltpu.VMEM((tokens, split), bf16),
            pltpu.VMEM((2, depth * n, ff), bf16),
            pltpu.VMEM((deep * n, width), bf16),
            dma((1,)), dma((1,)), dma((1,)), dma((1,)),
            dma((outer, 2)), dma((outer, 2)),
            dma((outer, 2)), dma((outer, 2)),
            dma((2 * outer, 2)), dma((2 * outer, 2)),
            dma((2 * outer, 2)), dma((2 * outer, 2)),
            pltpu.SemaphoreType.REGULAR((n.bit_length(),)),
        ],
        compiler_params=pltpu.CompilerParams(
            collective_id=0, has_side_effects=True, vmem_limit_bytes=VMEM_MIB * 1024 * 1024
        ),
    )(
        *(
            pltpu.with_memory_space_constraint(a, space)
            for a, space in zip(
                (
                    inputs, row_list, col_list.reshape(1, length), row_list.reshape(1, length), gain_attn.reshape(1, width),
                    w_qkv, w_out, gain_ffn.reshape(1, width), w_gate, w_up, w_down,
                ),
                (pltpu.HBM,) * 11,
            )
        )
    )
    return result.reshape(rows_here, length, width)


def solution(mesh):
    placed = (
        P("sample", "harm", None),
        P("sample"),
        P("sample"),
        P(),
        P(),
        P(),
        P(),
        P("harm", None),
        P("harm", None),
        P("harm", None),
    )
    return jax.shard_map(
        functools.partial(per_device, mesh.shape["harm"]),
        mesh=mesh, in_specs=placed, out_specs=P("harm", "sample", None), check_vma=False,
    )
```
